32 devices in a mesh: dp: 8 (over z, x), fsdp: 4 (over y, core).
Axes of the slice: x: 2, y: 2, z: 4, core: 2. Of those that a mesh axis runs over, the one named last changes fastest.
Arguments:
- tokens: bfloat16 [2, 16384, 1024], P(None, ('dp', 'fsdp')), may hold values from -6 to 6
- cotangent: bfloat16 [2, 16384, 1024], P(None, ('dp', 'fsdp')), may hold values from -6 to 6
- picks: int32 [2, 256, 16], P(None, ('dp', 'fsdp')), may hold values from 0 to 63, as said below
- pick_count: int32 [2, 256], P(None, ('dp', 'fsdp')), may hold values from 0 to 16, as said below
- first_length: int32 [2, 32], P(None, ('dp', 'fsdp')), may hold values from 256 to 512, as said below
- w_query: bfloat16 [1024, 1024], P('dp', 'fsdp'), may hold values from -0.1875 to 0.1875
- w_key: bfloat16 [1024, 1024], P('dp', 'fsdp'), may hold values from -0.1875 to 0.1875
- w_value: bfloat16 [1024, 1024], P('dp', 'fsdp'), may hold values from -0.1875 to 0.1875
- w_out: bfloat16 [1024, 1024], P('dp', 'fsdp'), may hold values from -0.5 to 0.5
- w_up: bfloat16 [1024, 4096], P('dp', 'fsdp'), may hold values from -0.1875 to 0.1875
- w_down: bfloat16 [4096, 1024], P('dp', 'fsdp'), may hold values from -0.09375 to 0.09375
- w_router: bfloat16 [1024], P('dp'), may hold values from -0.1875 to 0.1875
- gain_attn: bfloat16 [1024], P('dp'), may hold values from 0.25 to 1.75
- gain_mlp: bfloat16 [1024], P('dp'), may hold values from 0.25 to 1.75
Outputs:
- mixed: bfloat16 [2, 16384, 1024], P(None, ('dp', 'fsdp'))
- grad_tokens: bfloat16 [2, 16384, 1024], P(None, ('dp', 'fsdp'))
- grad_query: float32 [1024, 1024], P('dp', 'fsdp')
- grad_key: float32 [1024, 1024], P('dp', 'fsdp')
- grad_value: float32 [1024, 1024], P('dp', 'fsdp')
- grad_out: float32 [1024, 1024], P('dp', 'fsdp')
- grad_up: float32 [1024, 4096], P('dp', 'fsdp')
- grad_down: float32 [4096, 1024], P('dp', 'fsdp')
- grad_router: float32 [1024], P('dp')
- grad_gain_attn: float32 [1024], P('dp')
- grad_gain_mlp: float32 [1024], P('dp')
The draws below stay inside these ranges and needn't reach their ends.
Inputs may be any that keep to these rules, and one draw needn't show every extreme that they name: `picks`: within one piece the 16 offsets are distinct and increasing; only the first pick_count of them are routed. `pick_count`: each routed block receives exactly 64 routed tokens in all, and every sequence routes one eighth of its tokens. `first_length`: either 512 (one sequence) or 512 // 2 (two sequences of equal length).
All inputs are finite; a program needn't handle non-finite values.
Results may differ from the reference program's by a relative error of at most 0.011.
Values may be sent and summed in bfloat16 or wider, within the bound.
No kernel may reach another device: no remote copies, remote signals or barrier semaphores. Data moves between devices by JAX's collectives and lax.ppermute only.
A program may use at most 192 MiB of HBM per device.

```python
import jax
import jax.numpy as jnp
from jax import lax

D = 1024
HEAD_DIM = 64
FF = 4096
TOK_DEV = 512
MICRO = 2
ROUTERS = 8
GROUPS = 4
SPAN = 8
PIECE = 64
PIECE_CAP = 16
TOKENS = 16384
PICK_ROWS = 256


def pick_layout(key):
    base_key = jax.random.fold_in(key, 11)
    count_key = jax.random.fold_in(base_key, 1)
    order_key = jax.random.fold_in(base_key, 2)
    halves = jax.random.randint(count_key, (MICRO, ROUTERS // SPAN, SPAN // 2, GROUPS, SPAN), 0, PIECE_CAP + 1)
    halves = halves.at[:, :, 0].set(PIECE_CAP)
    counts = jnp.stack([halves, PIECE_CAP - halves], axis=3).reshape(MICRO, PICK_ROWS)
    scores = jax.random.randint(order_key, (MICRO, PICK_ROWS, PIECE), 0, 1 << 20)
    distinct = scores * PIECE + lax.broadcasted_iota(jnp.int32, (MICRO, PICK_ROWS, PIECE), 2)
    ordering = jnp.argsort(distinct, axis=-1, stable=True)[:, :, :PIECE_CAP]
    chosen = jnp.sort(ordering, axis=-1)
    return (chosen.astype(jnp.int32), counts.astype(jnp.int32))


def draw_picks(key, part):
    return pick_layout(key)[0]


def draw_pick_count(key, part):
    return pick_layout(key)[1]


def draw_first_length(key, part):
    choose_bits = jax.random.randint(jax.random.fold_in(key, 5), (MICRO, ROUTERS * GROUPS), 0, 2)
    choose_bits = choose_bits.at[:, 0].set(1).at[:, 1].set(0)
    if SPAN < 4:
        choose_bits = jnp.ones((MICRO, ROUTERS * GROUPS), jnp.int32)
    return jnp.where(choose_bits == 1, TOK_DEV, TOK_DEV // 2).astype(jnp.int32)


def steps_of(key, extent, pieces, least, top_value):
    factor_of, own = 1.0, jax.random.fold_in(key, 6)
    for dim, parts in pieces:
        draws = jnp.exp(jax.random.uniform(jax.random.fold_in(own, dim), (parts,), jnp.float32, least / len(pieces), top_value / len(pieces)))
        factor_of = factor_of * jnp.repeat(draws, extent[dim] // parts).reshape([-1 if axis == dim else 1 for axis in range(len(extent))])
    return factor_of


def centred(stream_key, shape, spread, limit, pieces=(), kind=jnp.bfloat16):
    factor_of = steps_of(stream_key, shape, pieces, -0.22, 0.18) if pieces else 1.0
    entries = jax.random.normal(stream_key, shape, jnp.float32) * spread * factor_of
    return jnp.minimum(jnp.maximum(entries, -limit), limit).astype(kind)


def setup_inputs(seed: int = 0) -> dict:
    arg_keys = jax.random.split(jax.random.key(seed), 15)
    tokens = centred(arg_keys[0], (MICRO, TOKENS, D), 1.0, 6.0, ((1, 32),))
    cotangent = centred(arg_keys[1], (MICRO, TOKENS, D), 1.0, 6.0, ((1, 32),))
    picks = draw_picks(jax.random.fold_in(arg_keys[14], 71), 0)
    pick_count = draw_pick_count(jax.random.fold_in(arg_keys[14], 71), 0)
    first_length = draw_first_length(jax.random.fold_in(arg_keys[14], 71), 0)
    w_query = centred(arg_keys[5], (D, D), D ** -0.5, 0.1875, ((0, 8), (1, 4)))
    w_key = centred(arg_keys[6], (D, D), D ** -0.5, 0.1875, ((0, 8), (1, 4)))
    w_value = centred(arg_keys[7], (D, D), D ** -0.5, 0.1875, ((0, 8), (1, 4)))
    w_out = centred(arg_keys[8], (D, D), (D // 8) ** -0.5, 0.5, ((0, 8), (1, 4)))
    w_up = centred(arg_keys[9], (D, FF), D ** -0.5, 0.1875, ((0, 8), (1, 4)))
    w_down = centred(arg_keys[10], (FF, D), FF ** -0.5, 0.09375, ((0, 8), (1, 4)))
    w_router = centred(arg_keys[11], (D,), D ** -0.5, 0.1875, ((0, 8),))
    gain_attn = jnp.clip(1.0 + 0.15 * jax.random.normal(arg_keys[12], (D,), jnp.float32), 0.25, 1.75).astype(jnp.bfloat16)
    gain_mlp = jnp.clip(1.0 + 0.15 * jax.random.normal(arg_keys[13], (D,), jnp.float32), 0.25, 1.75).astype(jnp.bfloat16)
    return {"tokens": tokens, "cotangent": cotangent, "picks": picks, "pick_count": pick_count, "first_length": first_length, "w_query": w_query, "w_key": w_key, "w_value": w_value, "w_out": w_out, "w_up": w_up, "w_down": w_down, "w_router": w_router, "gain_attn": gain_attn, "gain_mlp": gain_mlp}


@jax.custom_vjp
def low(v):
    return lax.optimization_barrier(v.astype(jnp.bfloat16)).astype(jnp.float32)

@jax.custom_vjp
def low_back(v):
    return v

def low_keep(v):
    return (low(v), None)

def low_pass(kept, grad):
    return (grad,)

def back_keep(v):
    return (v, None)

def back_low(kept, grad):
    return (low(grad),)
low.defvjp(low_keep, low_pass)
low_back.defvjp(back_keep, back_low)
EPSILON = 1e-06
SCORE_SCALE = 0.125
HIGHEST = lax.Precision.HIGHEST

def norm_apply(values, gain_vec):
    return values * lax.rsqrt(lax.optimization_barrier(jnp.mean(values * values, axis=-1, keepdims=True)) + EPSILON) * gain_vec

def matmul(left_op, right_op):
    return jnp.dot(left_op, right_op, precision=HIGHEST)

def layer(hidden, weight_set, position, sequence_id, is_live):
    w_query, w_key, w_value, w_out, w_up, w_down, w_router, gain_attn, gain_mlp = weight_set
    slot_count = hidden.shape[0]
    hidden = low_back(hidden)
    gate_value = jax.nn.sigmoid(matmul(hidden, w_router))
    normed = low(norm_apply(hidden, gain_attn))
    query_heads = low_back(low(matmul(normed, w_query))).reshape(slot_count, -1, HEAD_DIM)
    key_heads = low_back(low(matmul(normed, w_key))).reshape(slot_count, -1, HEAD_DIM)
    value_heads = low_back(low(matmul(normed, w_value))).reshape(slot_count, -1, HEAD_DIM)
    logits = low_back(jnp.einsum('qhe,khe->hqk', query_heads, key_heads, precision=HIGHEST) * SCORE_SCALE)
    allowed = is_live[None, :] & (sequence_id[:, None] == sequence_id[None, :]) & (position[None, :] <= position[:, None]) | jnp.eye(slot_count, dtype=jnp.bool_)
    logits = jnp.where(allowed[None], logits, -1e+30)
    row_peak = lax.optimization_barrier(jnp.max(logits, axis=-1, keepdims=True))
    exponent = jnp.exp(logits - row_peak)
    probability = exponent / lax.optimization_barrier(jnp.sum(exponent, axis=-1, keepdims=True))
    attended = jnp.einsum('hqk,khe->qhe', low(probability), value_heads, precision=HIGHEST).reshape(slot_count, -1)
    attended = low_back(low(attended))
    branch = low_back(matmul(attended, w_out))
    middle = hidden + branch
    normed_mlp = low(norm_apply(middle, gain_mlp))
    upper_act = low_back(matmul(normed_mlp, w_up))
    active = low(jax.nn.gelu(upper_act, approximate=False))
    lower_out = low_back(matmul(active, w_down))
    return low(gate_value[:, None] * (branch + lower_out))

def reference(tokens, cotangent, picks, pick_count, first_length, w_query, w_key, w_value, w_out, w_up, w_down, w_router, gain_attn, gain_mlp):
    weight_set = tuple((w.astype(jnp.float32) for w in (w_query, w_key, w_value, w_out, w_up, w_down, w_router, gain_attn, gain_mlp)))
    devices_all = ROUTERS * GROUPS
    block_total = MICRO * devices_all

    def one_block(totals, block_id):
        step_id = block_id // devices_all
        owner = block_id % devices_all
        owner_dp = owner // GROUPS
        group_id = owner % GROUPS
        base_dp = owner_dp // SPAN * SPAN
        piece_id = owner_dp % SPAN
        source = (base_dp + jnp.arange(SPAN, dtype=jnp.int32)) * GROUPS + group_id
        piece_rows = source * SPAN + piece_id
        offsets = picks[step_id, piece_rows]
        counts = pick_count[step_id, piece_rows]
        is_live = (jnp.arange(PIECE_CAP, dtype=jnp.int32)[None, :] < counts[:, None]).reshape(-1)
        row_ids = (source[:, None] * TOK_DEV + piece_id * PIECE + offsets).reshape(-1).astype(jnp.int32)
        position = (jnp.arange(SPAN, dtype=jnp.int32)[:, None] * PIECE + offsets).reshape(-1)
        sequence_id = (position >= first_length[step_id, owner]).astype(jnp.int32)
        inputs = tokens[step_id, row_ids].astype(jnp.float32)
        seed_grad = cotangent[step_id, row_ids].astype(jnp.float32) * is_live[:, None].astype(jnp.float32)
        delta, pullback = jax.vjp(lambda hidden, weights: layer(hidden, weights, position, sequence_id, is_live), inputs, weight_set)
        back_hidden, back_weights = pullback(seed_grad)
        totals = tuple((total + grad for total, grad in zip(totals, back_weights)))
        return (totals, (delta.astype(jnp.bfloat16), back_hidden.astype(jnp.bfloat16), row_ids, is_live))
    start = tuple((jnp.zeros(w.shape, jnp.float32) for w in weight_set))
    totals, (deltas, back_rows, row_ids, lives) = lax.scan(one_block, start, jnp.arange(block_total, dtype=jnp.int32))
    step_ids = jnp.broadcast_to((jnp.arange(block_total, dtype=jnp.int32) // devices_all)[:, None], row_ids.shape)
    keep_rows = lives[:, :, None]
    base_tokens = tokens[step_ids, row_ids]
    new_tokens = jnp.where(keep_rows, (base_tokens.astype(jnp.float32) + deltas.astype(jnp.float32)).astype(jnp.bfloat16), base_tokens)
    mixed = tokens.at[step_ids, row_ids].set(new_tokens)
    base_grads = cotangent[step_ids, row_ids]
    new_grads = jnp.where(keep_rows, (base_grads.astype(jnp.float32) + back_rows.astype(jnp.float32)).astype(jnp.bfloat16), base_grads)
    grad_tokens = cotangent.at[step_ids, row_ids].set(new_grads)
    return (mixed, grad_tokens, totals[0], totals[1], totals[2], totals[3], totals[4], totals[5], totals[6], totals[7], totals[8])
```

```python
import jax
import jax.numpy as jnp
from jax import lax
from jax.sharding import PartitionSpec as P

HEAD_DIM = 64
EPSILON = 1e-06
SCORE_SCALE = 0.125
BF16 = jnp.bfloat16
F32 = jnp.float32


def dot_nn(a, b):
    return lax.dot_general(a, b, (((1,), (0,)), ((), ())), preferred_element_type=F32)


def dot_nt(a, b):
    return lax.dot_general(a, b, (((1,), (1,)), ((), ())), preferred_element_type=F32)


def dot_tn(a, b):
    return lax.dot_general(a, b, (((0,), (0,)), ((), ())), preferred_element_type=F32)


def swap(value, axis, distance):
    return lax.ppermute(
        value, axis, [(i, i ^ distance) for i in range(lax.axis_size(axis))]
    )


def xor_order(value, axis, index, count):
    stride = 1
    while stride < count:
        shape = value.shape
        split = value.reshape(
            shape[:axis] + (count // (2 * stride), 2, stride) + shape[axis + 1 :]
        )
        flipped = jnp.flip(split, axis + 1).reshape(shape)
        value = jnp.where((index // stride) % 2 == 1, flipped, value)
        stride *= 2
    return value


def rstd_of(values):
    return lax.rsqrt(jnp.mean(values * values, axis=-1, keepdims=True) + EPSILON)


def norm_back(values, gain, grad):
    rstd = rstd_of(values)
    hat = values * rstd
    scaled = grad * gain
    back = rstd * (scaled - hat * jnp.mean(scaled * hat, axis=-1, keepdims=True))
    return back, jnp.sum(grad * hat, axis=0)


class Rows:
    def __init__(self):
        self.size = lax.axis_size("dp")
        self.me = lax.axis_index("dp")
        self.direct = self.size == 8

    def basis(self, value):
        if not self.direct:
            return value
        rows, width = value.shape
        parts = value.reshape(rows, self.size, width // self.size)
        return xor_order(parts, 1, self.me, self.size).reshape(rows, width)

    def gather(self, shard):
        if not self.direct:
            return lax.all_gather(shard, "dp", axis=0, tiled=True)
        line = jnp.stack([shard] + [swap(shard, "dp", 2 * d) for d in (1, 2, 3)])
        other = swap(line, "dp", 1)
        both = jnp.stack([line, other], axis=1)
        return both.reshape((-1,) + shard.shape[1:])

    def scatter(self, partial):
        if not self.direct:
            return lax.psum_scatter(partial, "dp", scatter_dimension=0, tiled=True)
        rows = partial.shape[0] // 8
        slots = partial.reshape((4, 2, rows) + partial.shape[1:])
        line = slots[:, 0] + swap(slots[:, 1].astype(BF16), "dp", 1).astype(F32)
        total = line[0]
        for d in (1, 2, 3):
            total = total + swap(line[d].astype(BF16), "dp", 2 * d).astype(F32)
        return total


def turn_pairs(size, groups, step):
    per = size // groups
    pairs = []
    for r in range(size):
        for j in range(groups):
            half = (r % per) ^ step
            pairs.append((r * groups + j, (j * per + half) * groups + r // per))
    return pairs


def turn(shard, me, size, groups):
    per = size // groups
    rows, cols = shard.shape
    parts = xor_order(shard.reshape(rows, per, cols // per), 1, me % per, per)
    got = [
        lax.ppermute(parts[:, t], ("dp", "fsdp"), turn_pairs(size, groups, t))
        for t in range(per)
    ]
    return xor_order(jnp.stack(got), 0, me % per, per).reshape(per * rows, cols // per).T


def turn_back(held, me, size, groups):
    per = size // groups
    whole = held.T
    parts = xor_order(whole.reshape((per, -1) + whole.shape[1:]), 0, me % per, per)
    got = []
    for t in range(per):
        pairs = [(b, a) for a, b in turn_pairs(size, groups, t)]
        got.append(lax.ppermute(parts[t].astype(BF16), ("dp", "fsdp"), pairs).astype(F32))
    mine = xor_order(jnp.stack(got, 1), 1, me % per, per)
    return mine.reshape(mine.shape[0], -1)


def group_all(own):
    pair = jnp.concatenate([own, swap(own, "fsdp", 2)])
    return jnp.concatenate([pair, swap(pair, "fsdp", 1)])


def near_all(pair):
    return jnp.concatenate([pair, swap(pair, "fsdp", 1)])


def near_sum(partial):
    half = partial.shape[0] // 2
    return partial[:half] + swap(partial[half:].astype(BF16), "fsdp", 1).astype(F32)


def far_sum(pair):
    half = pair.shape[0] // 2
    came = swap(pair.astype(BF16), "fsdp", 2).astype(F32)
    return pair + jnp.concatenate([came[half:], came[:half]])


def far_own(pair):
    half = pair.shape[0] // 2
    return pair[:half] + swap(pair[half:].astype(BF16), "fsdp", 2).astype(F32)


def attention_mask(first, live, span):
    row = lax.broadcasted_iota(jnp.int32, (live, live), 0)
    col = lax.broadcasted_iota(jnp.int32, (live, live), 1)
    edge = (first * live // span)[:, None, None]
    return (col <= row)[None] & ((row >= edge) == (col >= edge))


def body(
    tokens,
    cotangent,
    picks,
    pick_count,
    first_length,
    w_query,
    w_key,
    w_value,
    w_out,
    w_up,
    w_down,
    w_router,
    gain_attn,
    gain_mlp,
):
    move = Rows()
    size, me = move.size, move.me
    groups = lax.axis_size("fsdp")
    micro, tok_dev, width = tokens.shape
    span = picks.shape[1]
    cap = picks.shape[2]
    piece = tok_dev // span
    live = tok_dev // 8
    lane = me % span
    slots = span * cap

    picks_x = xor_order(picks, 1, lane, span)
    count_x = xor_order(pick_count, 1, lane, span)
    piece_x = lane ^ lax.broadcasted_iota(jnp.int32, (1, span, 1), 1)
    target = (piece_x * piece + picks_x).reshape(micro, slots)
    choose = (
        target[:, :, None] == lax.broadcasted_iota(jnp.int32, (1, 1, tok_dev), 2)
    ).astype(BF16)
    sent_live = (
        lax.broadcasted_iota(jnp.int32, (1, 1, cap), 2) < count_x[:, :, None]
    ).reshape(micro, slots)

    def pick(values):
        return jnp.einsum("mst,mtd->msd", choose, values, preferred_element_type=F32).astype(
            BF16
        )

    def exchange(values):
        parts = values.reshape(micro, span, -1, values.shape[-1])
        return jnp.stack(
            [parts[:, 0]] + [swap(parts[:, k], "dp", k) for k in range(1, span)], 1
        ).reshape(values.shape)

    got_tokens = exchange(pick(tokens))
    got_count = exchange(count_x[:, :, None]).reshape(micro, span)
    vectors = move.gather(jnp.stack([w_router, gain_attn, gain_mlp], 1).astype(BF16))
    w_qkv = move.gather(jnp.concatenate([w_query, w_key, w_value], 1))
    w_o = move.gather(turn(w_out, me, size, groups))
    w_u = move.gather(w_up)
    w_d = move.gather(turn(w_down, me, size, groups))
    got_cot = exchange(pick(cotangent))

    source = lane ^ lax.broadcasted_iota(jnp.int32, (span,), 0)
    before = (source[None, :] < source[:, None]).astype(jnp.int32)
    start = jnp.sum(before[None] * got_count[:, None, :], -1)
    nth = lax.broadcasted_iota(jnp.int32, (1, 1, cap), 2)
    rank = jnp.where(nth < got_count[:, :, None], start[:, :, None] + nth, -1)
    pack = (
        rank.reshape(micro, 1, slots) == lax.broadcasted_iota(jnp.int32, (1, live, 1), 1)
    ).astype(BF16)

    def packed(values):
        rows = jnp.einsum("mls,msd->mld", pack, values, preferred_element_type=F32)
        return move.basis(rows.astype(BF16).reshape(micro * live, width))

    def unpacked(values):
        rows = move.basis(values).reshape(micro, live, width)
        return jnp.einsum("mls,mld->msd", pack, rows, preferred_element_type=F32).astype(BF16)

    router = vectors[:, 0].astype(F32)
    gain_a = vectors[:, 1].astype(F32)
    gain_m = vectors[:, 2].astype(F32)
    own = micro * live
    first = first_length.reshape(micro)
    first_all = group_all(first[None]).reshape(-1)

    hidden = group_all(packed(got_tokens))
    h_all = hidden.astype(F32)
    normed = (h_all * rstd_of(h_all) * gain_a).astype(BF16)
    qkv = dot_nn(normed, w_qkv).astype(BF16)
    heads = qkv.shape[1] // 3 // HEAD_DIM
    units = groups * micro
    query, key, value = [
        x.reshape(units, live, heads, HEAD_DIM) for x in jnp.split(qkv, 3, axis=1)
    ]
    allowed = attention_mask(first_all, live, tok_dev)[:, None]
    logits = jnp.einsum("uqhe,ukhe->uhqk", query, key, preferred_element_type=F32) * SCORE_SCALE
    logits = jnp.where(allowed, logits, -1e30)
    exponent = jnp.exp(logits - jnp.max(logits, -1, keepdims=True))
    prob = exponent / jnp.sum(exponent, -1, keepdims=True)
    prob_low = prob.astype(BF16)
    attended = jnp.einsum("uhqk,ukhe->uqhe", prob_low, value, preferred_element_type=F32)
    attended = attended.reshape(groups * own, heads * HEAD_DIM).astype(BF16)
    branch = far_sum(near_sum(dot_nt(attended, w_o)))

    h_pair = h_all[: 2 * own]
    middle = h_pair + branch
    bnorm = near_all((middle * rstd_of(middle) * gain_m).astype(BF16))
    upper = dot_nn(bnorm, w_u)
    active = jax.nn.gelu(upper, approximate=False).astype(BF16)
    lower = far_sum(near_sum(dot_nt(active, w_d)))
    update = branch + lower
    gate = jax.nn.sigmoid(jnp.sum(h_pair * router, -1, keepdims=True))
    delta = (gate[:own] * update[:own]).astype(BF16)
    back_delta = exchange(unpacked(delta))

    cot_own = packed(got_cot)
    seed = jnp.concatenate([cot_own, swap(cot_own, "fsdp", 2)]).astype(F32)
    d_update = gate * seed
    d_score = (
        jnp.sum(seed[:own] * update[:own], -1, keepdims=True) * gate[:own] * (1.0 - gate[:own])
    )
    d_lower = near_all(d_update.astype(BF16))
    grad_down = dot_tn(d_lower, active)
    d_active = dot_nn(d_lower, w_d)
    _, gelu_pull = jax.vjp(lambda v: jax.nn.gelu(v, approximate=False), upper)
    d_upper = gelu_pull(d_active)[0].astype(BF16)
    d_bnorm = far_sum(near_sum(dot_nt(d_upper, w_u)))
    grad_up = dot_tn(bnorm, d_upper)
    d_middle, _ = norm_back(middle, gain_m, d_bnorm)
    _, g_gain_m = norm_back(middle[:own], gain_m, d_bnorm[:own])
    d_branch = near_all((d_update + d_middle).astype(BF16))
    d_att = dot_nn(d_branch, w_o).astype(BF16)
    grad_out = dot_tn(d_branch, attended)
    d_att = d_att.reshape(units, live, heads, HEAD_DIM)
    d_prob = jnp.einsum("uqhe,ukhe->uhqk", d_att, value, preferred_element_type=F32)
    d_logit = (prob * (d_prob - jnp.sum(d_prob * prob, -1, keepdims=True))).astype(BF16)
    d_query = jnp.einsum("uhqk,ukhe->uqhe", d_logit, key, preferred_element_type=F32) * SCORE_SCALE
    d_key = jnp.einsum("uhqk,uqhe->ukhe", d_logit, query, preferred_element_type=F32) * SCORE_SCALE
    d_value = jnp.einsum("uhqk,uqhe->ukhe", prob_low, d_att, preferred_element_type=F32)
    d_qkv = jnp.concatenate(
        [x.reshape(groups * own, -1).astype(BF16) for x in (d_query, d_key, d_value)], 1
    )
    d_normed = far_own(near_sum(dot_nt(d_qkv, w_qkv)))
    grad_qkv = dot_tn(normed, d_qkv)
    d_rows, g_gain_a = norm_back(h_all[:own], gain_a, d_normed)
    d_input = (d_middle[:own] + d_rows + d_score * router).astype(BF16)
    g_router = jnp.sum(d_score * h_all[:own], 0)
    back_grad = exchange(unpacked(d_input))

    put = choose * sent_live[:, :, None].astype(BF16)

    def place(base, rows):
        change = jnp.einsum("mst,msd->mtd", put, rows, preferred_element_type=F32)
        return (base.astype(F32) + change).astype(BF16)

    mixed = place(tokens, back_delta)
    grad_tokens = place(cotangent, back_grad)

    grad_up = move.scatter(grad_up)
    grad_down = turn_back(move.scatter(grad_down), me, size, groups)
    grad_out = turn_back(move.scatter(grad_out), me, size, groups)
    grad_query, grad_key, grad_value = jnp.split(move.scatter(grad_qkv), 3, axis=1)
    small = jnp.stack([g_router, g_gain_a, g_gain_m])
    small = small + swap(small, "fsdp", 1)
    small = small + swap(small, "fsdp", 2)
    if move.direct:
        small = small.reshape(3, size, -1)
        total = small[:, 0]
        for k in range(1, size):
            total = total + swap(small[:, k], "dp", k)
    else:
        total = lax.psum_scatter(small, "dp", scatter_dimension=1, tiled=True)
    return (
        mixed,
        grad_tokens,
        grad_query,
        grad_key,
        grad_value,
        grad_out,
        grad_up,
        grad_down,
        total[0],
        total[1],
        total[2],
    )


def solution(mesh):
    rows = P(None, ("dp", "fsdp"), None)
    flat = P(None, ("dp", "fsdp"))
    matrix = P("dp", "fsdp")
    vector = P("dp")
    return jax.shard_map(
        body,
        mesh=mesh,
        in_specs=(rows, rows, rows, flat, flat) + (matrix,) * 6 + (vector,) * 3,
        out_specs=(rows, rows) + (matrix,) * 6 + (vector,) * 3,
        check_vma=False,
    )
```

```python
import functools

import jax
import jax.numpy as jnp
from jax import lax
from jax.experimental import pallas as pl
from jax.experimental.pallas import tpu as pltpu
from jax.sharding import PartitionSpec as P

HEAD_DIM = 64
EPSILON = 1e-06
SCORE_SCALE = 0.125
DEAD = 64.0
BF16 = jnp.bfloat16
F32 = jnp.float32
SLOT_ORDER = (0, 4, 2, 6, 1, 5, 3, 7)


def dot_nn(a, b):
    return lax.dot_general(a, b, (((1,), (0,)), ((), ())), preferred_element_type=F32)


def dot_nt(a, b):
    return lax.dot_general(a, b, (((1,), (1,)), ((), ())), preferred_element_type=F32)


def dot_tn(a, b):
    return lax.dot_general(a, b, (((0,), (0,)), ((), ())), preferred_element_type=F32)


def swap(value, axis, distance):
    return lax.ppermute(
        value, axis, [(i, i ^ distance) for i in range(lax.axis_size(axis))]
    )


def xor_order(value, axis, index, count):
    stride = 1
    while stride < count:
        shape = value.shape
        split = value.reshape(
            shape[:axis] + (count // (2 * stride), 2, stride) + shape[axis + 1 :]
        )
        flipped = jnp.flip(split, axis + 1).reshape(shape)
        value = jnp.where((index // stride) % 2 == 1, flipped, value)
        stride *= 2
    return value


def rstd_of(values):
    return lax.rsqrt(jnp.mean(values * values, axis=-1, keepdims=True) + EPSILON)


def norm_back(values, gain, grad):
    rstd = rstd_of(values)
    hat = values * rstd
    scaled = grad * gain
    return rstd * (scaled - hat * jnp.mean(scaled * hat, axis=-1, keepdims=True)), grad * hat


def call(kernel, outs, args, smem=(), grid=None, in_specs=None, out_specs=None, scratch=(), flops=0):
    moved = sum(a.size * a.dtype.itemsize for a in args)
    moved += sum(s[0][0] * s[0][-1] * 4 for s in outs)
    whole = pl.BlockSpec(memory_space=pltpu.VMEM)
    scalar = pl.BlockSpec(memory_space=pltpu.SMEM)
    params = {} if grid is None else {"grid": grid}
    return pl.pallas_call(
        kernel,
        out_shape=[jax.ShapeDtypeStruct(shape, dtype) for shape, dtype in outs],
        in_specs=[scalar if i in smem else whole for i in range(len(args))]
        if in_specs is None
        else in_specs,
        out_specs=[whole] * len(outs) if out_specs is None else out_specs,
        scratch_shapes=list(scratch),
        cost_estimate=pl.CostEstimate(flops=flops, bytes_accessed=moved, transcendentals=0),
        **params,
    )(*args)


class Rows:
    def __init__(self):
        self.size = lax.axis_size("dp")
        self.me = lax.axis_index("dp")
        self.direct = self.size == 8

    def gather(self, shard):
        if not self.direct:
            whole = lax.all_gather(shard, "dp", axis=0, tiled=True)
            half = whole.shape[0] // 2
            return whole[:half], whole[half:]
        held = jnp.concatenate([shard, swap(shard, "dp", 4)])
        held = jnp.concatenate([held, swap(held, "dp", 2)])
        return held, swap(held, "dp", 1)

    def scatter(self, keep, send):
        if not self.direct:
            whole = jnp.concatenate([keep, send.astype(F32)])
            return lax.psum_scatter(whole, "dp", scatter_dimension=0, tiled=True)
        keep = keep + swap(send, "dp", 1).astype(F32)
        for distance in (2, 4):
            half = keep.shape[0] // 2
            came = swap(keep[half:].astype(BF16), "dp", distance)
            keep = keep[:half] + came.astype(F32)
        return keep


def lanes_apart(value, span):
    size = lax.axis_size("dp")
    lines = None
    if size != span:
        lines = [list(range(i, i + span)) for i in range(0, size, span)]
    return lax.all_to_all(value, "dp", 0, 0, tiled=True, axis_index_groups=lines)


def turn_pairs(size, groups, step):
    per = size // groups
    pairs = []
    for r in range(size):
        for j in range(groups):
            half = (r % per) ^ step
            pairs.append((r * groups + j, (j * per + half) * groups + r // per))
    return pairs


def turn(shards, me, size, groups):
    per = size // groups
    joined = jnp.concatenate(shards)
    rows, cols = joined.shape
    wide = cols // per
    got = []
    for t in range(per):
        part = lax.dynamic_slice(joined, (0, ((me % per) ^ t) * wide), (rows, wide))
        got.append(lax.ppermute(part, ("dp", "fsdp"), turn_pairs(size, groups, t)).T)
    ordered = xor_order(jnp.stack(got), 0, me % per, per)
    outs, start = [], 0
    for shard in shards:
        stop = start + shard.shape[0]
        outs.append(
            jnp.concatenate([ordered[t][:, start:stop] for t in range(per)], axis=1)
        )
        start = stop
    return outs


def turn_back(held, me, size, groups):
    per = size // groups
    parts = [xor_order(x.T.reshape((per, -1) + x.shape[:1]), 0, me % per, per) for x in held]
    joined = jnp.concatenate(parts, axis=1).astype(BF16)
    got = []
    for t in range(per):
        pairs = [(b, a) for a, b in turn_pairs(size, groups, t)]
        got.append(lax.ppermute(joined[t], ("dp", "fsdp"), pairs).astype(F32))
    mine = xor_order(jnp.stack(got, 1), 1, me % per, per)
    mine = mine.reshape(mine.shape[0], -1)
    outs, start = [], 0
    for part in parts:
        outs.append(mine[start : start + part.shape[1]])
        start += part.shape[1]
    return outs


def near_all(pair):
    return jnp.concatenate([pair, swap(pair, "fsdp", 1)])


def pick_kernel(target_ref, tok_ref, cot_ref, out_ref):
    target = target_ref[0]
    slots = target.shape[0]
    span, cap = out_ref.shape[0], out_ref.shape[3]
    rows = tok_ref.shape[1]
    choose = (target == lax.broadcasted_iota(jnp.int32, (slots, rows), 1)).astype(F32).astype(BF16)
    dead = jnp.where(target < 0, DEAD, 0.0).astype(F32)
    tok = (dot_nn(choose, tok_ref[0]) + dead).astype(BF16)
    cot = dot_nn(choose, cot_ref[0]).astype(BF16)
    for c in range(span):
        out_ref[c, 0, 0] = tok[c * cap : (c + 1) * cap]
        out_ref[c, 0, 1] = cot[c * cap : (c + 1) * cap]


def pick_rows(target, tokens, cotangent, span, cap):
    micro, rows, width = tokens.shape
    slots = span * cap
    return call(
        pick_kernel,
        [((span, micro, 2, cap, width), BF16)],
        [target.reshape(micro, slots, 1), tokens, cotangent],
        grid=(micro,),
        in_specs=[
            pl.BlockSpec((1, slots, 1), lambda m: (m, 0, 0)),
            pl.BlockSpec((1, rows, width), lambda m: (m, 0, 0)),
            pl.BlockSpec((1, rows, width), lambda m: (m, 0, 0)),
        ],
        out_specs=[pl.BlockSpec((span, 1, 2, cap, width), lambda m: (0, m, 0, 0, 0))],
        flops=4 * slots * rows * width,
    )[0]


def block_ids(index_ref, blocks):
    if blocks == 1:
        return [0]
    return [index_ref[0] ^ k for k in SLOT_ORDER]


def pack_kernel(live, blocks, index_ref, got_ref, hid_ref, cot_ref, pack_ref, wide_ref):
    span, micro, _, cap, width = got_ref.shape
    slots = span * cap
    block = width // blocks
    ids = block_ids(index_ref, blocks)
    below = lax.broadcasted_iota(jnp.int32, (slots, slots), 1) < lax.broadcasted_iota(
        jnp.int32, (slots, slots), 0
    )
    below = below.astype(F32).astype(BF16)
    for m in range(micro):
        tok = got_ref[:, m, 0].reshape(slots, width)
        alive = (tok[:, :128].astype(F32) < 0.5 * DEAD).astype(F32)
        rank = dot_nn(below, alive.astype(BF16))[:, :1].astype(jnp.int32)
        rank = jnp.where(alive[:, :1] > 0.5, rank, -1)
        pack = (rank == lax.broadcasted_iota(jnp.int32, (slots, live), 1)).astype(F32).astype(BF16)
        pack_ref[m] = pack
        for which, out_ref in ((0, hid_ref), (1, cot_ref)):
            rows = got_ref[:, m, which].reshape(slots, width)
            wide_ref[...] = dot_tn(pack, rows).astype(BF16)
            for s, i in enumerate(ids):
                start = i * block
                if blocks > 1:
                    start = pl.multiple_of(start, block)
                out_ref[m * live : (m + 1) * live, s * block : (s + 1) * block] = wide_ref[
                    :, pl.ds(start, block)
                ]


def softmax_of(query, key, allowed):
    logits = jnp.where(allowed, dot_nt(query, key) * SCORE_SCALE, -1e30)
    exponent = jnp.exp(logits - jnp.max(logits, -1, keepdims=True))
    return exponent / jnp.sum(exponent, -1, keepdims=True)


def allowed_of(edge_ref, block, own, live):
    row = lax.broadcasted_iota(jnp.int32, (own, own), 0)
    col = lax.broadcasted_iota(jnp.int32, (own, own), 1)
    micro = own // live
    edge = jnp.zeros((own, own), jnp.int32) + edge_ref[block * micro]
    for m in range(1, micro):
        edge = jnp.where(row >= m * live, edge_ref[block * micro + m], edge)
    late_row = (row % live >= edge).astype(jnp.int32)
    late_col = (col % live >= edge).astype(jnp.int32)
    return (row // live == col // live) & (col <= row) & (late_row == late_col)


def head_masks(own, cols):
    lane = lax.broadcasted_iota(jnp.int32, (own, cols), 1) // HEAD_DIM
    return [(lane == h).astype(F32) for h in range(cols // HEAD_DIM)]


def attend_kernel(live, edge_ref, hid_ref, vec_ref, w1_ref, w2_ref, norm_ref, qkv_ref, att_ref):
    rows, width = hid_ref.shape
    own = rows // 4
    half = width // 2
    cols = att_ref.shape[1]
    gain = vec_ref[1:2]
    masks = head_masks(own, cols)

    def step(b, _):
        at = pl.ds(pl.multiple_of(b * own, own), own)
        hid = hid_ref[at].astype(F32)
        normed = (hid * rstd_of(hid) * gain).astype(BF16)
        norm_ref[at] = normed
        qkv = dot_nn(normed[:, :half], w1_ref[:, : 3 * cols]) + dot_nn(
            normed[:, half:], w2_ref[:, : 3 * cols]
        )
        qkv = qkv.astype(BF16)
        qkv_ref[at] = qkv
        query, key, value = qkv[:, :cols], qkv[:, cols : 2 * cols], qkv[:, 2 * cols :]
        allowed = allowed_of(edge_ref, b, own, live)
        total = jnp.zeros((own, cols), F32)
        for mask in masks:
            prob = softmax_of(query * mask.astype(BF16), key, allowed).astype(BF16)
            total = total + dot_nn(prob, value) * mask
        att_ref[at] = total.astype(BF16)
        return 0

    lax.fori_loop(0, 4, step, 0)


def branch_kernel(att_ref, w1_ref, w2_ref, keep_ref, send_ref):
    half = w1_ref.shape[0]
    pair = keep_ref.shape[0]
    for at, ref in ((slice(0, pair), keep_ref), (slice(pair, 2 * pair), send_ref)):
        rows = att_ref[at]
        ref[:, :half] = dot_nt(rows, w1_ref[...]).astype(ref.dtype)
        ref[:, half:] = dot_nt(rows, w2_ref[...]).astype(ref.dtype)


def far_total(sum_ref, came_ref):
    own = sum_ref.shape[0] // 2
    came = jnp.concatenate([came_ref[own:], came_ref[:own]])
    return sum_ref[...] + came.astype(F32)


def middle_kernel(hid_ref, vec_ref, sum_ref, came_ref, branch_ref, middle_ref, norm_ref):
    branch = far_total(sum_ref, came_ref)
    middle = hid_ref[...].astype(F32) + branch
    branch_ref[...] = branch
    middle_ref[...] = middle
    norm_ref[...] = (middle * rstd_of(middle) * vec_ref[2:3]).astype(BF16)


def forward_kernel(norm_ref, u1_ref, u2_ref, d1_ref, d2_ref, act_ref, slope_ref, keep_ref, send_ref, acc_ref):
    half = u1_ref.shape[0]
    pair = keep_ref.shape[0]
    upper = dot_nn(norm_ref[:, :half], u1_ref[...]) + dot_nn(norm_ref[:, half:], u2_ref[...])
    phi = 0.5 + 0.5 * lax.erf(upper * 0.7071067811865476)
    active = (upper * phi).astype(BF16)
    act_ref[...] = active
    slope_ref[...] = phi + upper * (jnp.exp(-0.5 * upper * upper) * 0.3989422804014327)
    left, right = dot_nt(active, d1_ref[...]), dot_nt(active, d2_ref[...])

    @pl.when(pl.program_id(0) == 0)
    def _():
        acc_ref[:, :half] = left
        acc_ref[:, half:] = right

    @pl.when(pl.program_id(0) > 0)
    def _():
        acc_ref[:, :half] += left
        acc_ref[:, half:] += right

    @pl.when(pl.program_id(0) == pl.num_programs(0) - 1)
    def _():
        keep_ref[...] = acc_ref[:pair]
        send_ref[...] = acc_ref[pair:].astype(BF16)


def backward_kernel(low_ref, u1_ref, u2_ref, d1_ref, d2_ref, slope_ref, dup_ref, keep_ref, send_ref, acc_ref):
    half = u1_ref.shape[0]
    pair = keep_ref.shape[0]
    grad = dot_nn(low_ref[:, :half], d1_ref[...]) + dot_nn(low_ref[:, half:], d2_ref[...])
    grad = (grad * slope_ref[...]).astype(BF16)
    dup_ref[...] = grad
    left, right = dot_nt(grad, u1_ref[...]), dot_nt(grad, u2_ref[...])

    @pl.when(pl.program_id(0) == 0)
    def _():
        acc_ref[:, :half] = left
        acc_ref[:, half:] = right

    @pl.when(pl.program_id(0) > 0)
    def _():
        acc_ref[:, :half] += left
        acc_ref[:, half:] += right

    @pl.when(pl.program_id(0) == pl.num_programs(0) - 1)
    def _():
        keep_ref[...] = acc_ref[:pair]
        send_ref[...] = acc_ref[pair:].astype(BF16)


def feed(kernel, rows_in, weights, extra, outs_wide, tile):
    rows, width = rows_in.shape
    half, hidden = weights[0].shape
    fixed = pl.BlockSpec((rows, width), lambda i: (0, 0))
    weight = pl.BlockSpec((half, tile), lambda i: (0, i))
    wide = pl.BlockSpec((rows, tile), lambda i: (0, i))
    result = pl.BlockSpec((rows // 2, width), lambda i: (0, 0))
    return call(
        kernel,
        [((rows, hidden), dtype) for dtype in outs_wide]
        + [((rows // 2, width), F32), ((rows // 2, width), BF16)],
        [rows_in, *weights, *extra],
        grid=(hidden // tile,),
        in_specs=[fixed] + [weight] * 4 + [wide] * len(extra),
        out_specs=[wide] * len(outs_wide) + [result, result],
        scratch=[pltpu.VMEM((rows, width), F32)],
        flops=4 * rows * width * hidden,
    )


def update_kernel(hid_ref, vec_ref, sum_ref, came_ref, branch_ref, cot_ref, delta_ref, dup_ref, low_ref, score_ref):
    own = delta_ref.shape[0]
    update = branch_ref[...] + far_total(sum_ref, came_ref)
    hid = hid_ref[...].astype(F32)
    gate = jax.nn.sigmoid(jnp.sum(hid * vec_ref[0:1], -1, keepdims=True))
    delta_ref[...] = (gate * update)[:own].astype(BF16)
    seed = cot_ref[...].astype(F32)
    grad = gate * seed
    dup_ref[...] = grad
    low_ref[...] = grad.astype(BF16)
    score = jnp.sum(seed * update, -1, keepdims=True) * gate * (1.0 - gate)
    score_ref[...] = jnp.zeros(score_ref.shape, F32) + score[:own]


def turn_kernel(vec_ref, sum_ref, came_ref, mid_ref, dup_ref, dmid_ref, low_ref, gain_ref):
    own = dmid_ref.shape[0]
    back, term = norm_back(mid_ref[...], vec_ref[2:3], far_total(sum_ref, came_ref))
    dmid_ref[...] = back[:own]
    low_ref[...] = (dup_ref[...] + back).astype(BF16)
    gain_ref[...] = jnp.zeros(gain_ref.shape, F32) + jnp.sum(term[:own], 0, keepdims=True)


def attend_back_kernel(live, edge_ref, dbr_ref, o1_ref, o2_ref, w1_ref, w2_ref, qkv_ref, hid_ref, dqkv_ref, keep_ref, send_ref, gain_ref):
    rows, width = dbr_ref.shape
    own = rows // 4
    half = width // 2
    cols = o1_ref.shape[1]
    masks = head_masks(own, cols)
    gain_ref[...] = jnp.zeros(gain_ref.shape, F32)

    def step(b, out_ref, to):
        at = pl.ds(pl.multiple_of(b * own, own), own)
        dbr = dbr_ref[at]
        datt = (dot_nn(dbr[:, :half], o1_ref[...]) + dot_nn(dbr[:, half:], o2_ref[...])).astype(BF16)
        qkv = qkv_ref[at]
        query, key, value = qkv[:, :cols], qkv[:, cols : 2 * cols], qkv[:, 2 * cols :]
        allowed = allowed_of(edge_ref, b, own, live)
        dq = jnp.zeros((own, cols), F32)
        dk = jnp.zeros((own, cols), F32)
        dv = jnp.zeros((own, cols), F32)
        for mask in masks:
            low = mask.astype(BF16)
            prob = softmax_of(query * low, key, allowed)
            dprob = dot_nt(datt * low, value)
            dlog = (prob * (dprob - jnp.sum(dprob * prob, -1, keepdims=True))).astype(BF16)
            dq = dq + dot_nn(dlog, key) * mask
            dk = dk + dot_tn(dlog, query) * mask
            dv = dv + dot_tn(prob.astype(BF16), datt) * mask
        dq = (dq * SCORE_SCALE).astype(BF16)
        dk = (dk * SCORE_SCALE).astype(BF16)
        dqkv = jnp.concatenate([dq, dk, dv.astype(BF16)], 1)
        dqkv_ref[at] = dqkv
        hid = hid_ref[at].astype(F32)
        hat = hid * rstd_of(hid)
        for s, w_ref in ((slice(0, half), w1_ref), (slice(half, width), w2_ref)):
            part = dot_nt(dqkv, w_ref[:, : 3 * cols])
            gain_ref[:, s] += jnp.sum(part * hat[:, s], 0, keepdims=True)
            out_ref[to, s] = part.astype(out_ref.dtype)

    def keep_step(b, _):
        step(b, keep_ref, pl.ds(pl.multiple_of(b * own, own), own))
        return 0

    def send_step(b, _):
        step(b + 2, send_ref, pl.ds(pl.multiple_of(b * own, own), own))
        return 0

    lax.fori_loop(0, 2, send_step, 0)
    lax.fori_loop(0, 2, keep_step, 0)


def finish_kernel(live, blocks, index_ref, hid_ref, vec_ref, sum_ref, came_ref, dmid_ref, score_ref, delta_ref, pack_ref, out_ref, router_ref, wide_ref):
    micro, slots, _ = pack_ref.shape
    span, cap = out_ref.shape[0], out_ref.shape[3]
    own, width = delta_ref.shape
    block = width // blocks
    ids = block_ids(index_ref, blocks)
    hid = hid_ref[...].astype(F32)
    grad = sum_ref[...] + came_ref[...].astype(F32)
    back, _ = norm_back(hid, vec_ref[1:2], grad)
    score = score_ref[:, :1]
    router_ref[...] = jnp.zeros(router_ref.shape, F32) + jnp.sum(score * hid, 0, keepdims=True)
    grad_in = (dmid_ref[...] + back + score * vec_ref[0:1]).astype(BF16)
    for which, values in ((0, delta_ref[...]), (1, grad_in)):
        for s, i in enumerate(ids):
            start = i * block
            if blocks > 1:
                start = pl.multiple_of(start, block)
            wide_ref[:, pl.ds(start, block)] = values[:, s * block : (s + 1) * block]
        for m in range(micro):
            rows = dot_nn(pack_ref[m], wide_ref[m * live : (m + 1) * live]).astype(BF16)
            for c in range(span):
                out_ref[c, m, which] = rows[c * cap : (c + 1) * cap]


def place_kernel(target_ref, back_ref, tok_ref, cot_ref, mixed_ref, grad_ref):
    rows, width = tok_ref.shape[1:]
    span, cap = back_ref.shape[0], back_ref.shape[3]
    slots = span * cap
    put = (target_ref[0] == lax.broadcasted_iota(jnp.int32, (rows, slots), 0)).astype(F32).astype(BF16)
    for which, base_ref, out_ref in ((0, tok_ref, mixed_ref), (1, cot_ref, grad_ref)):
        change = dot_nn(put, back_ref[:, 0, which].reshape(slots, width))
        out_ref[0] = (base_ref[0].astype(F32) + change).astype(BF16)


def place_rows(target, back, tokens, cotangent):
    micro, rows, width = tokens.shape
    span, _, _, cap, _ = back.shape
    slots = span * cap
    full = pl.BlockSpec((1, rows, width), lambda m: (m, 0, 0))
    return call(
        place_kernel,
        [(tokens.shape, BF16), (tokens.shape, BF16)],
        [target.reshape(micro, 1, slots), back, tokens, cotangent],
        grid=(micro,),
        in_specs=[
            pl.BlockSpec((1, 1, slots), lambda m: (m, 0, 0)),
            pl.BlockSpec((span, 1, 2, cap, width), lambda m: (0, m, 0, 0, 0)),
            full,
            full,
        ],
        out_specs=[full, full],
        flops=4 * slots * rows * width,
    )


def halves(left, right):
    half = left.shape[1] // 2
    return dot_tn(left[:, :half], right), dot_tn(left[:, half:], right).astype(BF16)


def body(
    tokens,
    cotangent,
    picks,
    pick_count,
    first_length,
    w_query,
    w_key,
    w_value,
    w_out,
    w_up,
    w_down,
    w_router,
    gain_attn,
    gain_mlp,
):
    move = Rows()
    size, me = move.size, move.me
    groups = lax.axis_size("fsdp")
    micro, tok_dev, width = tokens.shape
    span, cap = picks.shape[1:]
    piece = tok_dev // span
    live = tok_dev // 8
    own = micro * live
    blocks = 8 if move.direct else 1
    index = me[None].astype(jnp.int32)

    nth = lax.broadcasted_iota(jnp.int32, picks.shape, 2)
    start = lax.broadcasted_iota(jnp.int32, picks.shape, 1) * piece
    target = jnp.where(nth < pick_count[:, :, None], start + picks, -1)
    target = target.reshape(micro, span * cap)
    sent = pick_rows(target, tokens, cotangent, span, cap)

    vectors = jnp.stack([w_router, gain_attn, gain_mlp], 1)
    pad = jnp.zeros((vectors.shape[0], 125), BF16)
    a_1, a_2 = move.gather(jnp.concatenate([w_query, w_key, w_value, vectors, pad], 1))
    turned_out, turned_down = turn([w_out, w_down], me, size, groups)
    heads_wide = turned_out.shape[1]
    hidden = w_up.shape[1]
    b_1, b_2 = move.gather(jnp.concatenate([turned_out, w_up], 1))
    d_1, d_2 = move.gather(turned_down)
    o_1, o_2 = b_1[:, :heads_wide], b_2[:, :heads_wide]
    u_1, u_2 = b_1[:, heads_wide:], b_2[:, heads_wide:]
    wide = 3 * heads_wide
    vec = jnp.concatenate([a_1[:, wide : wide + 8], a_2[:, wide : wide + 8]]).astype(F32).T

    got = lanes_apart(sent, span)
    hid_own, cot_own, pack = call(
        functools.partial(pack_kernel, live, blocks),
        [((own, width), BF16), ((own, width), BF16), ((micro, span * cap, live), BF16)],
        [index, got],
        smem=(0,),
        scratch=[pltpu.VMEM((live, width), BF16)],
    )
    first = (first_length.reshape(1, micro) * live // tok_dev).astype(jnp.int32)
    first = jnp.concatenate([first, swap(first, "fsdp", 2)])
    edges = jnp.concatenate([first, swap(first, "fsdp", 1)]).reshape(-1)
    hid_pair = jnp.concatenate([hid_own, swap(hid_own, "fsdp", 2)])
    hid = near_all(hid_pair)
    cot_pair = jnp.concatenate([cot_own, swap(cot_own, "fsdp", 2)])

    rows = groups * own
    normed, qkv, attended = call(
        functools.partial(attend_kernel, live),
        [((rows, width), BF16), ((rows, wide), BF16), ((rows, heads_wide), BF16)],
        [edges, hid, vec, a_1, a_2],
        smem=(0,),
        flops=2 * rows * width * wide,
    )
    half_outs = [((rows // 2, width), F32), ((rows // 2, width), BF16)]

    def far(keep, send):
        total = keep + swap(send, "fsdp", 1).astype(F32)
        return total, swap(total.astype(BF16), "fsdp", 2)

    total, came = far(
        *call(branch_kernel, half_outs, [attended, o_1, o_2], flops=2 * rows * width * heads_wide)
    )
    pair_f32 = ((rows // 2, width), F32)
    pair_low = ((rows // 2, width), BF16)
    branch, middle, bnorm = call(
        middle_kernel, [pair_f32, pair_f32, pair_low], [hid_pair, vec, total, came]
    )
    bnorm = near_all(bnorm)
    tile = min(256, hidden)
    active, slope, keep, send = feed(
        forward_kernel, bnorm, (u_1, u_2, d_1, d_2), (), (BF16, F32), tile
    )
    total, came = far(keep, send)
    delta, d_update, d_lower, score = call(
        update_kernel,
        [((own, width), BF16), pair_f32, pair_low, ((own, 128), F32)],
        [hid_pair, vec, total, came, branch, cot_pair],
    )
    d_lower = near_all(d_lower)
    d_upper, keep, send = feed(
        backward_kernel, d_lower, (u_1, u_2, d_1, d_2), (slope,), (BF16,), tile
    )
    total, came = far(keep, send)
    down_sum = move.scatter(*halves(d_lower, active))
    grad_up = move.scatter(*halves(bnorm, d_upper))
    d_middle, d_branch, gain_m = call(
        turn_kernel,
        [((own, width), F32), pair_low, ((8, width), F32)],
        [vec, total, came, middle, d_update],
    )
    d_branch = near_all(d_branch)
    d_qkv, keep, send, gain_a = call(
        functools.partial(attend_back_kernel, live),
        [((rows, wide), BF16)] + half_outs + [((8, width), F32)],
        [edges, d_branch, o_1, o_2, a_1, a_2, qkv, hid],
        smem=(0,),
        flops=2 * rows * width * wide,
    )
    total = keep + swap(send, "fsdp", 1).astype(F32)
    came = swap(total[own:].astype(BF16), "fsdp", 2)
    out, g_router = call(
        functools.partial(finish_kernel, live, blocks),
        [((span, micro, 2, cap, width), BF16), ((8, width), F32)],
        [index, hid_own, vec, total[:own], came, d_middle, score, delta, pack],
        smem=(0,),
        scratch=[pltpu.VMEM((own, width), BF16)],
    )
    back = lanes_apart(out, span)
    mixed, grad_tokens = place_rows(target, back, tokens, cotangent)

    keep_q, send_q = halves(normed, d_qkv)
    keep_o, send_o = halves(d_branch, attended)
    small = jnp.stack([g_router[0], gain_a[0], gain_m[0]], 1)
    small = jnp.concatenate([small, jnp.zeros((width, 125), F32)], 1)
    top = width // 2
    last = move.scatter(
        jnp.concatenate([keep_q, keep_o, small[:top]], 1),
        jnp.concatenate([send_q, send_o, small[top:].astype(BF16)], 1),
    )
    grad_query, grad_key, grad_value, out_sum, small = jnp.split(
        last, [heads_wide, 2 * heads_wide, wide, wide + heads_wide], axis=1
    )
    grad_out, grad_down = turn_back([out_sum, down_sum], me, size, groups)
    small = small[:, :8].T
    small = small + swap(small, "fsdp", 1)
    small = small + swap(small, "fsdp", 2)
    return (
        mixed,
        grad_tokens,
        grad_query,
        grad_key,
        grad_value,
        grad_out,
        grad_up,
        grad_down,
        small[0],
        small[1],
        small[2],
    )


def solution(mesh):
    rows = P(None, ("dp", "fsdp"), None)
    flat = P(None, ("dp", "fsdp"))
    matrix = P("dp", "fsdp")
    vector = P("dp")
    return jax.shard_map(
        body,
        mesh=mesh,
        in_specs=(rows, rows, rows, flat, flat) + (matrix,) * 6 + (vector,) * 3,
        out_specs=(rows, rows) + (matrix,) * 6 + (vector,) * 3,
        check_vma=False,
    )
```
